32 devices in a mesh: group: 2 (over x), seq: 8 (over z, y), head: 2 (over core).
Axes of the slice: x: 2, y: 2, z: 4, core: 2. Of those that a mesh axis runs over, the one named last changes fastest.
Arguments:
- queries: bfloat16 [4096, 8192], P(('group', 'seq', 'head')), parts along dimension 0, may hold values from -6 to 6
- keys: bfloat16 [4096, 1024], P(('group', 'seq', 'head')), parts along dimension 0, may hold values from -6 to 6
- values: bfloat16 [4096, 1024], P(('group', 'seq', 'head')), parts along dimension 0, may hold values from -6 to 6
- lengths: int32 [8], P('group'), parts along dimension 0, may hold values from 1 to 1024, 2048 in all
- assign: int32 [32], P('group'), parts along dimension 0, may hold values from 0 to 15, each once
Outputs:
- attended: bfloat16 [4096, 8192], P(('group', 'seq', 'head')), parts along dimension 0
The draws below stay inside these ranges and needn't reach their ends.
There are 2 independent parts, one for each index of `group`. The reference program is written for one: setup_inputs(seed, part) draws one part's arguments, and reference() takes and returns one part's arrays. A program takes and returns all parts, laid end to end along the dimension named above; each array names one. Nothing has to cross between parts.
Inputs may be any that keep to these rules, and one draw needn't show every extreme that they name: 4 positive lengths summing to 2048, the largest exactly 1024. `assign`: each span index once.
All inputs are finite; a program needn't handle non-finite values.
Results may differ from the reference program's by a relative error of at most 0.004.
Values may be sent and summed in bfloat16 or wider, within the bound.
No kernel may reach another device: no remote copies, remote signals or barrier semaphores. Data moves between devices by JAX's collectives and lax.ppermute only.
A program may use at most 128 MiB of HBM per device.

```python
import math
import jax
import jax.numpy as jnp
import numpy as np
from jax import lax

QUERY_HEADS = 64
KEY_VALUE_HEADS = 8
HEAD_SIZE = 128
TOK_DEV = 128
DOCS = 4
SPANS = 16
PACKED_TOKENS = 2048


def draw_queries(key, part):
    base_offset = jnp.clip(jax.random.normal(jax.random.fold_in(key, 11), (PACKED_TOKENS, QUERY_HEADS * HEAD_SIZE), jnp.float32), -6.0, 6.0)
    return base_offset.astype(jnp.bfloat16)


def draw_keys(key, part):
    base_offset = jnp.clip(jax.random.normal(jax.random.fold_in(key, 12), (PACKED_TOKENS, KEY_VALUE_HEADS * HEAD_SIZE), jnp.float32), -6.0, 6.0)
    return base_offset.astype(jnp.bfloat16)


def level_of(key, shape, cuts, low, high):
    loudness, own = 1.0, jax.random.fold_in(key, 6)
    for dim, shards_of in cuts:
        draws = jnp.exp(jax.random.uniform(jax.random.fold_in(own, dim), (shards_of,), jnp.float32, low / len(cuts), high / len(cuts)))
        loudness = loudness * jnp.repeat(draws, shape[dim] // shards_of).reshape([-1 if axis == dim else 1 for axis in range(len(shape))])
    return loudness


def split_up(number_of, total, limit, slope):
    portions = [(1 << 20) // math.isqrt(rank ** slope) + 1 for rank in range(2, number_of + 1)]
    surplus, holding = total - limit - (number_of - 1), [1] * (number_of - 1)
    while surplus > 0:
        candidates = [i for i in range(number_of - 1) if holding[i] < limit]
        mass, budget = sum([portions[i] for i in candidates]), surplus
        for i in candidates:
            addition = min(limit - holding[i], max(1, budget * portions[i] // mass), surplus)
            holding[i] = holding[i] + addition
            surplus = surplus - addition
    return np.array([limit] + holding)


def ragged_sizes(own_key, number_of, total, reach, lean):
    if number_of == 2:
        one = jax.random.randint(own_key, (), max(1, total - reach), min(reach, total - 1) + 1)
        return jnp.stack([one, total - one])
    sizes = jnp.asarray(split_up(number_of, total, reach, lean), jnp.int32)
    couples = (number_of - 1) // 2
    source_of, taker = sizes[1:1 + 2 * couples:2], sizes[2:2 + 2 * couples:2]
    margin = jnp.minimum(source_of - 1, reach - taker)
    moved = jax.random.randint(jax.random.fold_in(own_key, 1), (couples,), 0, 1 << 20) % (margin + 1)
    sizes = sizes.at[1:1 + 2 * couples:2].set(source_of - moved).at[2:2 + 2 * couples:2].set(taker + moved)
    return sizes[jax.random.permutation(jax.random.fold_in(own_key, 2), number_of)]


def scatter_about(rng, shape, deviation, reach, cuts=(), kind=jnp.bfloat16):
    entries = deviation * jax.random.normal(rng, shape, jnp.float32)
    if cuts:
        entries = entries * level_of(rng, shape, cuts, -0.22, 0.18)
    return jnp.clip(entries, -reach, reach).astype(kind)


def setup_inputs(seed: int = 0, part: int = 0) -> dict:
    splits = jax.random.split(jax.random.key(seed), 6)
    own_keys = jax.random.split(jax.random.fold_in(splits[5], part), 6)
    return {
        "queries": draw_queries(jax.random.fold_in(jax.random.fold_in(splits[5], part), 71), part),
        "keys": draw_keys(jax.random.fold_in(jax.random.fold_in(splits[5], part), 71), part),
        "values": scatter_about(own_keys[2], (PACKED_TOKENS, KEY_VALUE_HEADS * HEAD_SIZE), 1.0, 6.0, ((0, 16),)),
        "lengths": ragged_sizes(own_keys[3], DOCS, PACKED_TOKENS, PACKED_TOKENS // 2, 2).astype(jnp.int32),
        "assign": jax.random.permutation(own_keys[4], SPANS).astype(jnp.int32),
    }


def reference(queries, keys, values, lengths, assign):
    rows = jnp.arange(PACKED_TOKENS, dtype=jnp.int32)
    place = assign[rows // TOK_DEV].astype(jnp.int32) * TOK_DEV + rows % TOK_DEV
    ends = jnp.cumsum(lengths).astype(jnp.int32)
    owner = jnp.sum((place[:, None] >= ends[None, :]).astype(jnp.int32), axis=1)
    visible = (owner[:, None] == owner[None, :]) & (place[None, :] <= place[:, None])
    query_group = QUERY_HEADS // KEY_VALUE_HEADS
    scale = 1.0 / (HEAD_SIZE ** 0.5)
    q_heads = queries.reshape(PACKED_TOKENS, QUERY_HEADS, HEAD_SIZE).transpose(1, 0, 2)
    key_head_rows = keys.reshape(PACKED_TOKENS, KEY_VALUE_HEADS, HEAD_SIZE).transpose(1, 0, 2)
    value_head_rows = values.reshape(PACKED_TOKENS, KEY_VALUE_HEADS, HEAD_SIZE).transpose(1, 0, 2)

    def one_head(head):
        query = q_heads[head]
        key = key_head_rows[head // query_group]
        value = value_head_rows[head // query_group]
        scores = jnp.dot(query, key.T, preferred_element_type=jnp.float32) * scale
        scores = jnp.where(visible, scores, -jnp.inf)
        top = jnp.max(scores, axis=1, keepdims=True)
        weights = jnp.exp(scores - top)
        total = jnp.sum(weights, axis=1, keepdims=True)
        return jnp.dot(weights.astype(jnp.bfloat16), value, preferred_element_type=jnp.float32) / total

    result = lax.map(one_head, jnp.arange(QUERY_HEADS, dtype=jnp.int32))
    return result.transpose(1, 0, 2).reshape(PACKED_TOKENS, QUERY_HEADS * HEAD_SIZE).astype(jnp.bfloat16)
```

```python
import functools
import math

import jax
import jax.numpy as jnp
from jax import lax
from jax.experimental import pallas as pl
from jax.experimental.pallas import tpu as pltpu
from jax.sharding import PartitionSpec as P

HEAD_SIZE = 128
AXES = ("seq", "head")
HIDDEN = -1e30


def ring_of(mesh):
    count = mesh.shape["seq"]
    places = []
    for device in mesh.devices[0, :, 0].flat:
        places.append(tuple(getattr(device, "coords", ())))
    if len(set(places)) == count:
        varied = [axis for axis in range(len(places[0])) if len({place[axis] for place in places}) > 1]
        for narrow in varied:
            sides = sorted({place[narrow] for place in places})
            if len(varied) == 2 and len(sides) == 2:
                long = [axis for axis in varied if axis != narrow][0]
                up = sorted((p[long], i) for i, p in enumerate(places) if p[narrow] == sides[0])
                down = sorted((p[long], i) for i, p in enumerate(places) if p[narrow] == sides[1])
                return [i for _, i in up] + [i for _, i in reversed(down)]
    return list(range(count))


def attend_kernel(blocks, first, last, span, docs, kv_heads, query_group, *refs):
    meta, ends, q_ref = refs[:3]
    k_refs, v_refs = refs[3 : 3 + blocks], refs[3 + blocks : 3 + 2 * blocks]
    refs = refs[3 + 2 * blocks :]
    if not first:
        acc_in, top_in, sum_in = refs[:3]
        refs = refs[3:]
    if last:
        (out_ref,) = refs[:1]
        refs = refs[1:]
    else:
        acc_out, top_out, sum_out = refs[:3]
        refs = refs[3:]
    bias, k_picked, v_picked = refs

    own = meta[0]
    factor = math.log2(math.e) / math.sqrt(HEAD_SIZE)
    row = own * span + lax.broadcasted_iota(jnp.int32, (span, span), 0)
    begin = jnp.zeros((span, span), jnp.int32)
    low = jnp.int32(0)
    for d in range(docs):
        begin = jnp.where(row >= ends[d], ends[d], begin)
        low = jnp.where(own * span >= ends[d], ends[d], low)

    place = [meta[1 + b] for b in range(blocks)]
    seen = [((p <= own) & (p * span + span > low)).astype(jnp.int32) for p in place]
    before = []
    count = jnp.int32(0)
    for b in range(blocks):
        before.append(count)
        count = count + seen[b]
    choice, spot = [], []
    for j in range(blocks):
        index, where = jnp.int32(0), jnp.int32(0)
        for b in range(blocks):
            hit = (seen[b] == 1) & (before[b] == j)
            index = jnp.where(hit, b, index)
            where = jnp.where(hit, place[b], where)
        choice.append(index)
        spot.append(where)

    def work(shown):
        for j in range(shown):
            column = spot[j] * span + lax.broadcasted_iota(jnp.int32, (span, span), 1)
            ok = (column >= begin) & (column <= row)
            bias[:, j * span : (j + 1) * span] = jnp.where(ok, 0.0, HIDDEN)

        def one_key_head(g, carry):
            at = pl.ds(pl.multiple_of(g * HEAD_SIZE, HEAD_SIZE), HEAD_SIZE)
            for j in range(shown):
                for picked, sources in ((k_picked, k_refs), (v_picked, v_refs)):
                    tile = sources[0][:, at]
                    for b in range(1, blocks):
                        tile = jnp.where(choice[j] == b, sources[b][:, at], tile)
                    picked[j * span : (j + 1) * span, :] = tile
            for h in range(query_group):
                here = pl.ds(
                    pl.multiple_of((g * query_group + h) * HEAD_SIZE, HEAD_SIZE), HEAD_SIZE
                )
                if shown:
                    scores = lax.dot_general(
                        q_ref[:, here],
                        k_picked[: shown * span, :],
                        (((1,), (1,)), ((), ())),
                        preferred_element_type=jnp.float32,
                    )
                    scores = scores + bias[:, : shown * span]
                    highest = jnp.max(scores, axis=1, keepdims=True)
                    highest = jnp.broadcast_to(highest * factor, (span, HEAD_SIZE))
                    if not first:
                        older = top_in[:, here]
                        highest = jnp.maximum(highest, older)
                    shift = jnp.concatenate([highest] * shown, axis=1) if shown > 1 else highest
                    weights = jnp.exp2(scores * factor - shift)
                    part = weights[:, :span]
                    for j in range(1, shown):
                        part = part + weights[:, j * span : (j + 1) * span]
                    product = jnp.dot(
                        weights.astype(jnp.bfloat16),
                        v_picked[: shown * span, :],
                        preferred_element_type=jnp.float32,
                    )
                    if not first:
                        fade = jnp.exp2(older - highest)
                        part = part + fade * sum_in[:, here]
                        product = product + fade * acc_in[:, here]
                else:
                    part, product = sum_in[:, here], acc_in[:, here]
                if last:
                    total = jnp.sum(part, axis=1, keepdims=True)
                    out_ref[:, here] = (product / total).astype(out_ref.dtype)
                else:
                    sum_out[:, here] = part
                    acc_out[:, here] = product
                    if shown:
                        top_out[:, here] = highest
            return carry

        lax.fori_loop(0, kv_heads, one_key_head, 0)

    for shown in range(1 if first else 0, blocks + 1):
        if shown == 0 and not last:
            continue
        pl.when(count == shown)(functools.partial(work, shown))


def attend(meta, ends, queries, keys, values, state, last, span, kv_heads):
    blocks = len(keys)
    first = state is None
    query_group = queries.shape[1] // (kv_heads * HEAD_SIZE)
    docs = ends.shape[0]
    wide = jax.ShapeDtypeStruct(queries.shape, jnp.float32)
    vmem = pl.BlockSpec(memory_space=pltpu.VMEM)
    smem = pl.BlockSpec(memory_space=pltpu.SMEM)
    inputs = [meta, ends, queries, *keys, *values] + ([] if first else list(state))
    aliases = {}
    if not first and not last:
        aliases = {3 + 2 * blocks + i: i for i in range(3)}
    area = span * span * blocks * kv_heads * query_group
    return pl.pallas_call(
        functools.partial(attend_kernel, blocks, first, last, span, docs, kv_heads, query_group),
        out_shape=jax.ShapeDtypeStruct(queries.shape, jnp.bfloat16) if last else (wide,) * 3,
        in_specs=[smem, smem] + [vmem] * (len(inputs) - 2),
        out_specs=vmem if last else (vmem,) * 3,
        scratch_shapes=[
            pltpu.VMEM((span, span * blocks), jnp.float32),
            pltpu.VMEM((span * blocks, HEAD_SIZE), jnp.bfloat16),
            pltpu.VMEM((span * blocks, HEAD_SIZE), jnp.bfloat16),
        ],
        input_output_aliases=aliases,
        cost_estimate=pl.CostEstimate(
            flops=2 * area * HEAD_SIZE, bytes_accessed=4 * queries.size, transcendentals=area // 2
        ),
        compiler_params=pltpu.CompilerParams(vmem_limit_bytes=16 << 20),
        name="attend",
    )(*inputs)


def solution(mesh):
    ring = ring_of(mesh)
    chips = len(ring)
    cores = mesh.shape["head"]
    spot = {seq: i for i, seq in enumerate(ring)}

    def along(step):
        return [
            (ring[i] * cores + c, ring[(i + step) % chips] * cores + c)
            for i in range(chips)
            for c in range(cores)
        ]

    def across(turn):
        return [
            (s * cores + c, s * cores + (c + turn) % cores)
            for s in range(chips)
            for c in range(cores)
        ]

    forward, backward = along(1), along(-1)

    def source(me, core, step, turn):
        seq = ring[(spot[me] - step) % chips]
        return seq * cores + (core - turn) % cores

    steps = list(range(1, (chips + 1) // 2))
    whole_order = [(0, t) for t in range(cores)]
    for s in steps:
        whole_order += [(d, t) for d in (s, -s) for t in range(cores)]
    if chips % 2 == 0:
        whole_order += [(chips // 2, t) for t in range(cores)]
    table = [
        [source(me, core, d, t) for d, t in whole_order] for me in range(chips) for core in range(cores)
    ]

    def local(queries, keys, values, lengths, assign):
        span = queries.shape[0]
        kv_heads = keys.shape[1] // HEAD_SIZE
        ends = jnp.cumsum(lengths)
        mine = lax.axis_index(AXES)
        order = lax.dynamic_index_in_dim(jnp.array(table, jnp.int32), mine, 0, keepdims=False)
        spans = jnp.arange(assign.shape[0], dtype=jnp.int32)
        places = jnp.sum(jnp.where(order[:, None] == spans[None, :], assign[None, :], 0), axis=1)

        def shared(array):
            return [array] + [lax.ppermute(array, AXES, across(t)) for t in range(1, cores)]

        def call(state, begin, keys, values, last=False):
            meta = jnp.concatenate([places[:1], places[begin : begin + len(keys)]])
            return attend(meta, ends, queries, keys, values, state, last, span, kv_heads)

        state = call(None, 0, shared(keys), shared(values))
        at = cores
        kf = kb = keys
        vf = vb = values
        for _ in steps:
            kf, kb = lax.ppermute(kf, AXES, forward), lax.ppermute(kb, AXES, backward)
            vf, vb = lax.ppermute(vf, AXES, forward), lax.ppermute(vb, AXES, backward)
            state = call(state, at, shared(kf) + shared(kb), shared(vf) + shared(vb))
            at += 2 * cores
        kf, vb = lax.ppermute(kf, AXES, forward), lax.ppermute(vb, AXES, backward)
        return call(state, at, shared(kf), shared(vb), last=True)

    placed = P(("group", "seq", "head"), None)
    return jax.shard_map(
        local,
        mesh=mesh,
        in_specs=(placed, placed, placed, P("group"), P("group")),
        out_specs=placed,
        check_vma=False,
    )
```

```python
import functools
import math

import jax
import jax.numpy as jnp
from jax import lax
from jax.experimental import pallas as pl
from jax.experimental.pallas import tpu as pltpu
from jax.sharding import PartitionSpec as P


HEAD_SIZE = 128
AXES = ("seq", "head")
HIDDEN = -1e30
LANES = 128


def ring_of(mesh):
    count = mesh.shape["seq"]
    places = []
    for device in mesh.devices[0, :, 0].flat:
        places.append(tuple(getattr(device, "coords", ())))
    if len(set(places)) == count:
        varied = [axis for axis in range(len(places[0])) if len({place[axis] for place in places}) > 1]
        for narrow in varied:
            sides = sorted({place[narrow] for place in places})
            if len(varied) == 2 and len(sides) == 2:
                long = [axis for axis in varied if axis != narrow][0]
                up = sorted((p[long], i) for i, p in enumerate(places) if p[narrow] == sides[0])
                down = sorted((p[long], i) for i, p in enumerate(places) if p[narrow] == sides[1])
                return [i for _, i in up] + [i for _, i in reversed(down)]
    return list(range(count))


def longest(wide, most):
    _, depth = wide.shape
    place = lax.broadcasted_iota(jnp.int32, (depth, LANES), 0) // HEAD_SIZE
    member = (place == lax.broadcasted_iota(jnp.int32, (depth, LANES), 1)).astype(jnp.bfloat16)
    wide = wide.astype(jnp.float32)
    squares = jnp.dot((wide * wide).astype(jnp.bfloat16), member, preferred_element_type=jnp.float32)
    return squares if most is None else jnp.maximum(most, squares)


def shift_kernel(kv_heads, q_ref, k_ref, v_ref, info_ref, shift_out):
    wide = q_ref.shape[1] // kv_heads
    k_long = jnp.max(longest(k_ref[...], None))
    q_long = None
    for g in range(kv_heads):
        q_long = longest(q_ref[:, g * wide : (g + 1) * wide], q_long)
    product = jnp.full(shift_out.shape, jnp.max(q_long), jnp.float32) * k_long
    shift_out[...] = jnp.maximum(jnp.sqrt(product) * 1.02, 1e-3)


def shift_of(queries, keys, values, info, kv_heads):
    vmem = pl.BlockSpec(memory_space=pltpu.VMEM)
    return pl.pallas_call(
        functools.partial(shift_kernel, kv_heads),
        out_shape=jax.ShapeDtypeStruct((8, LANES), jnp.float32),
        in_specs=[vmem, vmem, vmem, pl.BlockSpec(memory_space=pltpu.SMEM)],
        out_specs=vmem,
        cost_estimate=pl.CostEstimate(
            flops=4 * queries.size * LANES, bytes_accessed=2 * queries.size, transcendentals=0
        ),
        compiler_params=pltpu.CompilerParams(vmem_limit_bytes=16 << 20),
        name="shift",
    )(queries, keys, values, info)


def attend_kernel(table, at, tail, part_of, blocks, spare, first, last, span, docs, kv_heads, query_group, *refs):
    info, q_ref = refs[:2]
    k_refs, v_refs = refs[2 : 2 + blocks], refs[2 + blocks : 2 + 2 * blocks]
    refs = refs[2 + 2 * blocks :]
    spare_k, spare_v = refs[:spare], refs[spare : 2 * spare]
    refs = refs[2 * spare :]
    shift_in = refs[0]
    refs = refs[1:]
    if last:
        least = refs[0]
        refs = refs[1:]
    if not first:
        acc_in, sum_in = refs[:2]
        refs = refs[2:]
    if last:
        out_ref = refs[0]
        refs = refs[1:]
    else:
        acc_out, sum_out = refs[:2]
        refs = refs[2:]
        if first:
            least = refs[0]
            refs = refs[1:]
    bias, values2 = refs[:2]
    wide = query_group * HEAD_SIZE
    if last:
        most_ref, all_k, all_v, sem, result, out_sem, places = refs[2:]

    mine = lax.axis_index("seq") * lax.axis_size("head") + lax.axis_index("head")

    def place_of(b):
        stored = jnp.int32(table[0][b])
        for device in range(1, len(table)):
            if table[device][b] != table[0][b]:
                stored = jnp.where(mine == device, table[device][b], stored)
        return info[docs + stored]

    own = place_of(0)
    factor = math.log2(math.e) / math.sqrt(HEAD_SIZE)
    place = [place_of(b) for b in at]
    ends = [info[0]]
    for d in range(1, docs):
        ends.append(ends[-1] + info[d])

    def begin_of(row):
        begin = jnp.zeros_like(row)
        for d in range(docs):
            begin = jnp.where(row >= ends[d], ends[d], begin)
        return begin

    def head_at(g, h):
        return pl.ds(pl.multiple_of((g * query_group + h) * HEAD_SIZE, HEAD_SIZE), HEAD_SIZE)

    shift = shift_in[0:1, :]
    low = begin_of(own * span + jnp.zeros((), jnp.int32))

    def sees(b):
        p = place_of(b)
        return ((p <= own) & (p * span + span > low)).astype(jnp.int32)

    seen = [sees(b) for b in at]
    if tail is not None:
        mine_now, swapped_now, final = tail
        n_mine = sum(sees(b) for b in mine_now)
        n_swapped = sum(sees(b) for b in swapped_now)
        n_final = sum(sees(b) for b in final)
        lone = (n_mine == 1) & (n_swapped == 1) & (n_final == 2)
        early = ((n_mine > 0) & jnp.logical_not(lone)).astype(jnp.int32)
        late = ((n_swapped == 1) & (n_final <= 1)).astype(jnp.int32)
        for i, b in enumerate(at):
            if last:
                seen[i] = seen[i] * (late if b in swapped_now else 1)
            elif len(at) == len(mine_now):
                seen[i] = seen[i] * early
            else:
                seen[i] = seen[i] * (1 - late) * (1 - early if b in mine_now else 1)
    before = []
    count = jnp.int32(0)
    for b in range(blocks):
        before.append(count)
        count = count + seen[b]

    def chosen(j):
        index, where = jnp.int32(0), jnp.int32(1 << 20)
        for b in range(blocks):
            hit = (seen[b] == 1) & (before[b] == j)
            index = jnp.where(hit, b, index)
            where = jnp.where(hit, place[b] * span, where)
        return index, where

    row = own * span + lax.broadcasted_iota(jnp.int32, (span, span), 0)
    begin = begin_of(row)
    minus = -factor * shift

    values2[:, HEAD_SIZE:] = jnp.ones((2 * span, HEAD_SIZE), jnp.bfloat16)
    if last:
        most_ref[...] = jnp.zeros((span, HEAD_SIZE), jnp.float32)

    def send_out(g):
        part = pl.ds(pl.multiple_of(g * wide, wide), wide)
        return pltpu.make_async_copy(result.at[:, part], out_ref.at[:, part], out_sem.at[g])

    low_g, high_g = (kv_heads * i // part_of[1] for i in (part_of[0], part_of[0] + 1))

    def two_blocks(pair, carry):
        picks = []
        for i in range(2):
            index, where = chosen(2 * pair + i)
            picks.append(index)
            column = where + lax.broadcasted_iota(jnp.int32, (span, span), 1)
            ok = (column >= begin) & (column <= row)
            bias[:, i * span : (i + 1) * span] = jnp.where(ok, minus, HIDDEN)

        def one_key_head(g, carry):
            at = pl.ds(pl.multiple_of(g * HEAD_SIZE, HEAD_SIZE), HEAD_SIZE)
            sides = []
            for sources in (k_refs, v_refs):
                tiles = []
                for i in range(2):
                    tile = sources[0][:, at]
                    for b in range(1, blocks):
                        tile = jnp.where(picks[i] == b, sources[b][:, at], tile)
                    tiles.append(tile)
                sides.append(jnp.concatenate(tiles, axis=0))
            sides[1] = jnp.concatenate([sides[1], values2[:, HEAD_SIZE:]], axis=1)
            heads = range(query_group)
            q_rows = jnp.concatenate([q_ref[:, head_at(g, h)] for h in heads], axis=0)
            scores = lax.dot_general(
                q_rows,
                sides[0],
                (((1,), (1,)), ((), ())),
                preferred_element_type=jnp.float32,
            )
            offset = jnp.concatenate([bias[...]] * query_group, axis=0)
            weights = jnp.exp2(scores * factor + offset).astype(jnp.bfloat16)
            product = jnp.dot(weights, sides[1], preferred_element_type=jnp.float32)
            if last:
                largest = most_ref[...]
            if first:
                smallest = least[...]
            for h in heads:
                here = head_at(g, h)
                part = product[h * span : (h + 1) * span, :HEAD_SIZE]
                total = product[h * span : (h + 1) * span, HEAD_SIZE:]
                if last:
                    part, total = part + acc_in[:, here], total + sum_in[:, here]
                    result[:, here] = (part / total).astype(result.dtype)
                    largest = jnp.maximum(largest, total)
                elif first:
                    smallest = jnp.minimum(smallest, total)
                    acc_out[:, here], sum_out[:, here] = part, total
                else:
                    acc_out[:, here] = acc_out[:, here] + part
                    sum_out[:, here] = sum_out[:, here] + total
            if first:
                least[...] = smallest
            if last:
                most_ref[...] = largest
                send_out(g).start()
            return carry

        lax.fori_loop(low_g, high_g, one_key_head, 0, unroll=True)
        return carry

    if first:
        least[...] = jnp.full(least.shape, 1.0, jnp.float32)
        two_blocks(0, 0)
    elif last:

        @pl.when(count > 0)
        def _():
            two_blocks(0, 0)

        @pl.when(count == 0)
        def _():
            def divide(g, carry):
                largest = most_ref[...]
                for h in range(query_group):
                    here = head_at(g, h)
                    total = sum_in[:, here]
                    result[:, here] = (acc_in[:, here] / total).astype(result.dtype)
                    largest = jnp.maximum(largest, total)
                most_ref[...] = largest
                send_out(g).start()
                return carry

            lax.fori_loop(0, kv_heads, divide, 0)
    else:
        lax.fori_loop(0, (count + 1) // 2, two_blocks, 0)

    if last:
        fair = (least[...] >= 2.0**-90) & (most_ref[...] <= 1.0)
        good = jnp.min(jnp.where(fair, 1.0, 0.0)) > 0.5
        for g in range(kv_heads):
            send_out(g).wait()

        @pl.when(jnp.logical_not(good))
        def _():
            for b in range(spare):
                places[b] = place_of(b)
            tall_row = own * span + lax.broadcasted_iota(jnp.int32, (span, span), 0)
            tall_begin = begin_of(tall_row)

            def one_key_head(g, carry):
                at = pl.ds(pl.multiple_of(g * HEAD_SIZE, HEAD_SIZE), HEAD_SIZE)
                for b in range(spare):
                    for source, target in ((spare_k[b], all_k), (spare_v[b], all_v)):
                        copy = pltpu.make_async_copy(
                            source.at[:, at], target.at[b * span : (b + 1) * span, :], sem
                        )
                        copy.start()
                        copy.wait()

                def one_head(h, carry):
                    here = head_at(g, h)

                    def one_block(b, state):
                        top, total, part = state
                        tall = pl.ds(pl.multiple_of(b * span, span), span)
                        column = places[b] * span + lax.broadcasted_iota(
                            jnp.int32, (span, span), 1
                        )
                        ok = (column >= tall_begin) & (column <= tall_row)
                        scores = lax.dot_general(
                            q_ref[:, here],
                            all_k[tall, :],
                            (((1,), (1,)), ((), ())),
                            preferred_element_type=jnp.float32,
                        )
                        scores = jnp.where(ok, scores * factor, HIDDEN)
                        newer = jnp.maximum(top, jnp.max(scores, axis=1, keepdims=True))
                        weights = jnp.where(ok, jnp.exp2(scores - newer), 0.0)
                        fade = jnp.exp2(top - newer)
                        total = total * fade + jnp.sum(weights, axis=1, keepdims=True)
                        part = part * fade + jnp.dot(
                            weights.astype(jnp.bfloat16),
                            all_v[tall, :],
                            preferred_element_type=jnp.float32,
                        )
                        return newer, total, part

                    start = (
                        jnp.full((span, 1), HIDDEN, jnp.float32),
                        jnp.zeros((span, 1), jnp.float32),
                        jnp.zeros((span, HEAD_SIZE), jnp.float32),
                    )
                    _, total, part = lax.fori_loop(0, spare, one_block, start)
                    result[:, here] = (part / total).astype(result.dtype)
                    return carry

                lax.fori_loop(0, query_group, one_head, 0)
                send_out(g).start()
                send_out(g).wait()
                return carry

            lax.fori_loop(0, kv_heads, one_key_head, 0)


def attend(table, at, tail, part_of, info, queries, keys, values, shift, state, every, docs, span, kv_heads):
    blocks = len(keys)
    first, last = state is None, every is not None
    spare = len(every[0]) if last else 0
    query_group = queries.shape[1] // (kv_heads * HEAD_SIZE)
    wide = jax.ShapeDtypeStruct(queries.shape, jnp.float32)
    vmem = pl.BlockSpec(memory_space=pltpu.VMEM)
    smem = pl.BlockSpec(memory_space=pltpu.SMEM)
    loose = pl.BlockSpec(memory_space=pl.ANY)
    inputs = [info, queries, *keys, *values]
    specs = [smem] + [vmem] * (1 + 2 * blocks)
    if last:
        inputs += [*every[0], *every[1]]
        specs += [loose] * (2 * spare)
    inputs += [shift] + ([] if first else [state[2]] * last + list(state[:2]))
    specs += [vmem] * (1 if first else 3 + last)
    aliases = {}
    if last:
        shapes, outs = jax.ShapeDtypeStruct(queries.shape, jnp.bfloat16), loose
    else:
        shapes, outs = (wide, wide), (vmem,) * 2
        if first:
            shapes += (jax.ShapeDtypeStruct((span, HEAD_SIZE), jnp.float32),)
            outs = (vmem,) * 3
        else:
            base = 3 + 2 * blocks
            aliases = {base: 0, base + 1: 1}
    scratch = [
        pltpu.VMEM((span, 2 * span), jnp.float32),
        pltpu.VMEM((2 * span, 2 * HEAD_SIZE), jnp.bfloat16),
    ]
    if last:
        scratch += [
            pltpu.VMEM((span, HEAD_SIZE), jnp.float32),
            pltpu.VMEM((span * spare, HEAD_SIZE), jnp.bfloat16),
            pltpu.VMEM((span * spare, HEAD_SIZE), jnp.bfloat16),
            pltpu.SemaphoreType.DMA,
            pltpu.VMEM(queries.shape, jnp.bfloat16),
            pltpu.SemaphoreType.DMA((kv_heads,)),
            pltpu.SMEM((spare,), jnp.int32),
        ]
    area = span * span * blocks * kv_heads * query_group
    result = pl.pallas_call(
        functools.partial(
            attend_kernel, table, at, tail, part_of, blocks, spare, first, last, span, docs, kv_heads, query_group
        ),
        out_shape=shapes,
        in_specs=specs,
        out_specs=outs,
        scratch_shapes=scratch,
        input_output_aliases=aliases,
        cost_estimate=pl.CostEstimate(
            flops=2 * area * HEAD_SIZE, bytes_accessed=4 * queries.size, transcendentals=area // 2
        ),
        compiler_params=pltpu.CompilerParams(vmem_limit_bytes=16 << 20),
        name="attend",
    )(*inputs)
    return result if first or last else (*result, state[2])


def solution(mesh):
    ring = ring_of(mesh)
    chips = len(ring)
    cores = mesh.shape["head"]
    spot = {seq: i for i, seq in enumerate(ring)}

    def along(step):
        return [
            (ring[i] * cores + c, ring[(i + step) % chips] * cores + c)
            for i in range(chips)
            for c in range(cores)
        ]

    def across(turn):
        return [
            (s * cores + c, s * cores + (c + turn) % cores)
            for s in range(chips)
            for c in range(cores)
        ]

    forward, backward = along(1), along(-1)

    def source(me, core, step, turn):
        seq = ring[(spot[me] - step) % chips]
        return seq * cores + (core - turn) % cores

    steps = list(range(1, (chips + 1) // 2))
    whole_order = [(0, t) for t in range(cores)]
    for s in steps:
        whole_order += [(d, t) for d in (s, -s) for t in range(cores)]
    if chips % 2 == 0:
        whole_order += [(chips // 2, t) for t in range(cores)]
    table = [
        [source(me, core, d, t) for d, t in whole_order] for me in range(chips) for core in range(cores)
    ]

    def local(queries, keys, values, lengths, assign):
        span = queries.shape[0]
        kv_heads = keys.shape[1] // HEAD_SIZE
        info = jnp.concatenate([lengths, assign])
        docs = lengths.shape[0]
        every = [[None] * len(table[0]), [None] * len(table[0])]

        def send(array, pairs):
            return lax.ppermute(array, AXES, pairs)

        def shared(array):
            return [array] + [send(array, across(t)) for t in range(1, cores)]

        def call(state, at, tail=None, part_of=(0, 1), last=False):
            keys, values = [every[0][b] for b in at], [every[1][b] for b in at]
            return attend(
                table,
                at,
                tail,
                part_of,
                info,
                queries,
                keys,
                values,
                shift,
                state,
                every if last else None,
                docs,
                span,
                kv_heads,
            )

        shift = shift_of(queries, keys, values, info, kv_heads)

        def arrived(begin, keys, values):
            every[0][begin : begin + len(keys)] = keys
            every[1][begin : begin + len(values)] = values
            return tuple(range(begin, begin + len(keys)))

        at = arrived(0, shared(keys), shared(values))
        state = call(None, at)
        kf = kb = keys
        vf = vb = values
        for s in steps:
            kf, kb = send(kf, forward), send(kb, backward)
            vf, vb = send(vf, forward), send(vb, backward)
            at = arrived(at[-1] + 1, shared(kf) + shared(kb), shared(vf) + shared(vb))
            if s < steps[-1]:
                state = call(state, at)
        s = steps[-1] + 1
        kf, vb = send(kf, forward), send(vb, backward)
        final = arrived(at[-1] + 1, shared(kf), shared(vb))
        mine_now = tuple(b for b in at if (b - at[0]) % cores == 0)
        swapped_now = tuple(b for b in at if b not in mine_now)
        tail = (mine_now, swapped_now, final)
        state = call(state, mine_now, tail)
        for i in (0, 1):
            state = call(state, at, tail, (i, 2))
        return call(state, swapped_now + final, tail, last=True)


    placed = P(("group", "seq", "head"), None)
    return jax.shard_map(
        local,
        mesh=mesh,
        in_specs=(placed, placed, placed, P("group"), P("group")),
        out_specs=placed,
        check_vma=False,
    )
```

```python
import functools
import math

import jax
import jax.numpy as jnp
from jax import lax
from jax.experimental import pallas as pl
from jax.experimental.pallas import tpu as pltpu
from jax.sharding import PartitionSpec as P


HEAD_SIZE = 128
AXES = ("seq", "head")
HIDDEN = -1e30
LANES = 128


def ring_of(mesh):
    count = mesh.shape["seq"]
    places = []
    for device in mesh.devices[0, :, 0].flat:
        places.append(tuple(getattr(device, "coords", ())))
    if len(set(places)) == count:
        varied = [axis for axis in range(len(places[0])) if len({place[axis] for place in places}) > 1]
        for narrow in varied:
            sides = sorted({place[narrow] for place in places})
            if len(varied) == 2 and len(sides) == 2:
                long = [axis for axis in varied if axis != narrow][0]
                up = sorted((p[long], i) for i, p in enumerate(places) if p[narrow] == sides[0])
                down = sorted((p[long], i) for i, p in enumerate(places) if p[narrow] == sides[1])
                return [i for _, i in up] + [i for _, i in reversed(down)]
    return list(range(count))


def longest(wide, most):
    _, depth = wide.shape
    place = lax.broadcasted_iota(jnp.int32, (depth, LANES), 0) // HEAD_SIZE
    member = (place == lax.broadcasted_iota(jnp.int32, (depth, LANES), 1)).astype(jnp.bfloat16)
    wide = wide.astype(jnp.float32)
    squares = jnp.dot((wide * wide).astype(jnp.bfloat16), member, preferred_element_type=jnp.float32)
    return squares if most is None else jnp.maximum(most, squares)


def shift_kernel(kv_heads, q_ref, k_ref, v_ref, info_ref, shift_out):
    wide = q_ref.shape[1] // kv_heads
    k_long = jnp.max(longest(k_ref[...], None))
    q_long = None
    for g in range(kv_heads):
        q_long = longest(q_ref[:, g * wide : (g + 1) * wide], q_long)
    product = jnp.full(shift_out.shape, jnp.max(q_long), jnp.float32) * k_long
    shift_out[...] = jnp.maximum(jnp.sqrt(product) * 1.02, 1e-3)


def shift_of(queries, keys, values, info, kv_heads):
    vmem = pl.BlockSpec(memory_space=pltpu.VMEM)
    return pl.pallas_call(
        functools.partial(shift_kernel, kv_heads),
        out_shape=jax.ShapeDtypeStruct((8, LANES), jnp.float32),
        in_specs=[vmem, vmem, vmem, pl.BlockSpec(memory_space=pltpu.SMEM)],
        out_specs=vmem,
        cost_estimate=pl.CostEstimate(
            flops=4 * queries.size * LANES, bytes_accessed=2 * queries.size, transcendentals=0
        ),
        compiler_params=pltpu.CompilerParams(vmem_limit_bytes=16 << 20),
        name="shift",
    )(queries, keys, values, info)


def attend_kernel(table, at, tail, part_of, blocks, spare, first, last, span, docs, kv_heads, query_group, *refs):
    info, q_ref = refs[:2]
    k_refs, v_refs = refs[2 : 2 + blocks], refs[2 + blocks : 2 + 2 * blocks]
    refs = refs[2 + 2 * blocks :]
    spare_k, spare_v = refs[:spare], refs[spare : 2 * spare]
    refs = refs[2 * spare :]
    shift_in = refs[0]
    refs = refs[1:]
    if last:
        least = refs[0]
        refs = refs[1:]
    if not first:
        acc_in, sum_in = refs[:2]
        refs = refs[2:]
    if last:
        out_ref = refs[0]
        refs = refs[1:]
    else:
        acc_out, sum_out = refs[:2]
        refs = refs[2:]
        if first:
            least = refs[0]
            refs = refs[1:]
    bias, values2 = refs[:2]
    wide = query_group * HEAD_SIZE
    if last:
        most_ref, all_k, all_v, sem, result, out_sem, places = refs[2:]

    mine = lax.axis_index("seq") * lax.axis_size("head") + lax.axis_index("head")

    def place_of(b):
        stored = jnp.int32(table[0][b])
        for device in range(1, len(table)):
            if table[device][b] != table[0][b]:
                stored = jnp.where(mine == device, table[device][b], stored)
        return info[docs + stored]

    own = place_of(0)
    factor = math.log2(math.e) / math.sqrt(HEAD_SIZE)
    place = [place_of(b) for b in at]
    ends = [info[0]]
    for d in range(1, docs):
        ends.append(ends[-1] + info[d])

    def begin_of(row):
        begin = jnp.zeros_like(row)
        for d in range(docs):
            begin = jnp.where(row >= ends[d], ends[d], begin)
        return begin

    def head_at(g, h):
        return pl.ds(pl.multiple_of((g * query_group + h) * HEAD_SIZE, HEAD_SIZE), HEAD_SIZE)

    shift = shift_in[0:1, :]
    low = begin_of(own * span + jnp.zeros((), jnp.int32))

    def sees(b):
        p = place_of(b)
        return ((p <= own) & (p * span + span > low)).astype(jnp.int32)

    seen = [sees(b) for b in at]
    if tail is not None:
        mine_now, swapped_now, final = tail
        n_mine = sum(sees(b) for b in mine_now)
        n_swapped = sum(sees(b) for b in swapped_now)
        n_final = sum(sees(b) for b in final)
        early = ((n_mine == 2) | ((n_mine == 1) & (n_swapped != 1))).astype(jnp.int32)
        rest = (1 - early) * n_mine + n_swapped
        late = ((rest == 1) & (n_final == 1)).astype(jnp.int32)
        for i, b in enumerate(at):
            if last:
                seen[i] = seen[i] * (late if b in swapped_now else 1)
            elif len(at) == len(mine_now):
                seen[i] = seen[i] * early
            else:
                seen[i] = seen[i] * (1 - late) * (1 - early if b in mine_now else 1)
    before = []
    count = jnp.int32(0)
    for b in range(blocks):
        before.append(count)
        count = count + seen[b]

    def chosen(j):
        index, where = jnp.int32(0), jnp.int32(1 << 20)
        for b in range(blocks):
            hit = (seen[b] == 1) & (before[b] == j)
            index = jnp.where(hit, b, index)
            where = jnp.where(hit, place[b] * span, where)
        return index, where

    row = own * span + lax.broadcasted_iota(jnp.int32, (span, span), 0)
    begin = begin_of(row)
    minus = -factor * shift

    values2[:, HEAD_SIZE:] = jnp.ones((2 * span, HEAD_SIZE), jnp.bfloat16)
    if last:
        most_ref[...] = jnp.zeros((span, HEAD_SIZE), jnp.float32)

    def send_out(g):
        part = pl.ds(pl.multiple_of(g * wide, wide), wide)
        return pltpu.make_async_copy(result.at[:, part], out_ref.at[:, part], out_sem.at[g])

    low_g, high_g = (kv_heads * i // part_of[1] for i in (part_of[0], part_of[0] + 1))

    def two_blocks(pair, carry):
        picks = []
        for i in range(2):
            index, where = chosen(2 * pair + i)
            picks.append(index)
            column = where + lax.broadcasted_iota(jnp.int32, (span, span), 1)
            ok = (column >= begin) & (column <= row)
            bias[:, i * span : (i + 1) * span] = jnp.where(ok, minus, HIDDEN)

        def one_key_head(g, carry):
            at = pl.ds(pl.multiple_of(g * HEAD_SIZE, HEAD_SIZE), HEAD_SIZE)
            sides = []
            for sources in (k_refs, v_refs):
                tiles = []
                for i in range(2):
                    tile = sources[0][:, at]
                    for b in range(1, blocks):
                        tile = jnp.where(picks[i] == b, sources[b][:, at], tile)
                    tiles.append(tile)
                sides.append(jnp.concatenate(tiles, axis=0))
            sides[1] = jnp.concatenate([sides[1], values2[:, HEAD_SIZE:]], axis=1)
            heads = range(query_group)
            q_rows = jnp.concatenate([q_ref[:, head_at(g, h)] for h in heads], axis=0)
            scores = lax.dot_general(
                q_rows,
                sides[0],
                (((1,), (1,)), ((), ())),
                preferred_element_type=jnp.float32,
            )
            offset = jnp.concatenate([bias[...]] * query_group, axis=0)
            weights = jnp.exp2(scores * factor + offset).astype(jnp.bfloat16)
            product = jnp.dot(weights, sides[1], preferred_element_type=jnp.float32)
            if last:
                largest = most_ref[...]
            if first:
                smallest = least[...]
            for h in heads:
                here = head_at(g, h)
                part = product[h * span : (h + 1) * span, :HEAD_SIZE]
                total = product[h * span : (h + 1) * span, HEAD_SIZE:]
                if last:
                    part, total = part + acc_in[:, here], total + sum_in[:, here]
                    result[:, here] = (part / total).astype(result.dtype)
                    largest = jnp.maximum(largest, total)
                elif first:
                    smallest = jnp.minimum(smallest, total)
                    acc_out[:, here], sum_out[:, here] = part, total
                else:
                    acc_out[:, here] = acc_out[:, here] + part
                    sum_out[:, here] = sum_out[:, here] + total
            if first:
                least[...] = smallest
            if last:
                most_ref[...] = largest
                send_out(g).start()
            return carry

        lax.fori_loop(low_g, high_g, one_key_head, 0, unroll=True)
        return carry

    if first:
        least[...] = jnp.full(least.shape, 1.0, jnp.float32)
        two_blocks(0, 0)
    elif last:

        @pl.when(count > 0)
        def _():
            two_blocks(0, 0)

        @pl.when(count == 0)
        def _():
            def divide(g, carry):
                largest = most_ref[...]
                for h in range(query_group):
                    here = head_at(g, h)
                    total = sum_in[:, here]
                    result[:, here] = (acc_in[:, here] / total).astype(result.dtype)
                    largest = jnp.maximum(largest, total)
                most_ref[...] = largest
                send_out(g).start()
                return carry

            lax.fori_loop(0, kv_heads, divide, 0)
    else:
        lax.fori_loop(0, (count + 1) // 2, two_blocks, 0)

    if last:
        fair = (least[...] >= 2.0**-90) & (most_ref[...] <= 1.0)
        good = jnp.min(jnp.where(fair, 1.0, 0.0)) > 0.5
        for g in range(kv_heads):
            send_out(g).wait()

        @pl.when(jnp.logical_not(good))
        def _():
            for b in range(spare):
                places[b] = place_of(b)
            tall_row = own * span + lax.broadcasted_iota(jnp.int32, (span, span), 0)
            tall_begin = begin_of(tall_row)

            def one_key_head(g, carry):
                at = pl.ds(pl.multiple_of(g * HEAD_SIZE, HEAD_SIZE), HEAD_SIZE)
                for b in range(spare):
                    for source, target in ((spare_k[b], all_k), (spare_v[b], all_v)):
                        copy = pltpu.make_async_copy(
                            source.at[:, at], target.at[b * span : (b + 1) * span, :], sem
                        )
                        copy.start()
                        copy.wait()

                def one_head(h, carry):
                    here = head_at(g, h)

                    def one_block(b, state):
                        top, total, part = state
                        tall = pl.ds(pl.multiple_of(b * span, span), span)
                        column = places[b] * span + lax.broadcasted_iota(
                            jnp.int32, (span, span), 1
                        )
                        ok = (column >= tall_begin) & (column <= tall_row)
                        scores = lax.dot_general(
                            q_ref[:, here],
                            all_k[tall, :],
                            (((1,), (1,)), ((), ())),
                            preferred_element_type=jnp.float32,
                        )
                        scores = jnp.where(ok, scores * factor, HIDDEN)
                        newer = jnp.maximum(top, jnp.max(scores, axis=1, keepdims=True))
                        weights = jnp.where(ok, jnp.exp2(scores - newer), 0.0)
                        fade = jnp.exp2(top - newer)
                        total = total * fade + jnp.sum(weights, axis=1, keepdims=True)
                        part = part * fade + jnp.dot(
                            weights.astype(jnp.bfloat16),
                            all_v[tall, :],
                            preferred_element_type=jnp.float32,
                        )
                        return newer, total, part

                    start = (
                        jnp.full((span, 1), HIDDEN, jnp.float32),
                        jnp.zeros((span, 1), jnp.float32),
                        jnp.zeros((span, HEAD_SIZE), jnp.float32),
                    )
                    _, total, part = lax.fori_loop(0, spare, one_block, start)
                    result[:, here] = (part / total).astype(result.dtype)
                    return carry

                lax.fori_loop(0, query_group, one_head, 0)
                send_out(g).start()
                send_out(g).wait()
                return carry

            lax.fori_loop(0, kv_heads, one_key_head, 0)


def attend(table, at, tail, part_of, info, queries, keys, values, shift, state, every, docs, span, kv_heads):
    blocks = len(keys)
    first, last = state is None, every is not None
    spare = len(every[0]) if last else 0
    query_group = queries.shape[1] // (kv_heads * HEAD_SIZE)
    wide = jax.ShapeDtypeStruct(queries.shape, jnp.float32)
    vmem = pl.BlockSpec(memory_space=pltpu.VMEM)
    smem = pl.BlockSpec(memory_space=pltpu.SMEM)
    loose = pl.BlockSpec(memory_space=pl.ANY)
    inputs = [info, queries, *keys, *values]
    specs = [smem] + [vmem] * (1 + 2 * blocks)
    if last:
        inputs += [*every[0], *every[1]]
        specs += [loose] * (2 * spare)
    inputs += [shift] + ([] if first else [state[2]] * last + list(state[:2]))
    specs += [vmem] * (1 if first else 3 + last)
    aliases = {}
    if last:
        shapes, outs = jax.ShapeDtypeStruct(queries.shape, jnp.bfloat16), loose
    else:
        shapes, outs = (wide, wide), (vmem,) * 2
        if first:
            shapes += (jax.ShapeDtypeStruct((span, HEAD_SIZE), jnp.float32),)
            outs = (vmem,) * 3
        else:
            base = 3 + 2 * blocks
            aliases = {base: 0, base + 1: 1}
    scratch = [
        pltpu.VMEM((span, 2 * span), jnp.float32),
        pltpu.VMEM((2 * span, 2 * HEAD_SIZE), jnp.bfloat16),
    ]
    if last:
        scratch += [
            pltpu.VMEM((span, HEAD_SIZE), jnp.float32),
            pltpu.VMEM((span * spare, HEAD_SIZE), jnp.bfloat16),
            pltpu.VMEM((span * spare, HEAD_SIZE), jnp.bfloat16),
            pltpu.SemaphoreType.DMA,
            pltpu.VMEM(queries.shape, jnp.bfloat16),
            pltpu.SemaphoreType.DMA((kv_heads,)),
            pltpu.SMEM((spare,), jnp.int32),
        ]
    area = span * span * blocks * kv_heads * query_group
    result = pl.pallas_call(
        functools.partial(
            attend_kernel, table, at, tail, part_of, blocks, spare, first, last, span, docs, kv_heads, query_group
        ),
        out_shape=shapes,
        in_specs=specs,
        out_specs=outs,
        scratch_shapes=scratch,
        input_output_aliases=aliases,
        cost_estimate=pl.CostEstimate(
            flops=2 * area * HEAD_SIZE, bytes_accessed=4 * queries.size, transcendentals=area // 2
        ),
        compiler_params=pltpu.CompilerParams(vmem_limit_bytes=16 << 20),
        name="attend",
    )(*inputs)
    return result if first or last else (*result, state[2])


def solution(mesh):
    ring = ring_of(mesh)
    chips = len(ring)
    cores = mesh.shape["head"]
    spot = {seq: i for i, seq in enumerate(ring)}

    def along(step):
        return [
            (ring[i] * cores + c, ring[(i + step) % chips] * cores + c)
            for i in range(chips)
            for c in range(cores)
        ]

    def across(turn):
        return [
            (s * cores + c, s * cores + (c + turn) % cores)
            for s in range(chips)
            for c in range(cores)
        ]

    forward, backward = along(1), along(-1)

    def source(me, core, step, turn):
        seq = ring[(spot[me] - step) % chips]
        return seq * cores + (core - turn) % cores

    steps = list(range(1, (chips + 1) // 2))
    whole_order = [(0, t) for t in range(cores)]
    for s in steps:
        whole_order += [(d, t) for d in (s, -s) for t in range(cores)]
    if chips % 2 == 0:
        whole_order += [(chips // 2, t) for t in range(cores)]
    table = [
        [source(me, core, d, t) for d, t in whole_order] for me in range(chips) for core in range(cores)
    ]

    def local(queries, keys, values, lengths, assign):
        span = queries.shape[0]
        kv_heads = keys.shape[1] // HEAD_SIZE
        info = jnp.concatenate([lengths, assign])
        docs = lengths.shape[0]
        every = [[None] * len(table[0]), [None] * len(table[0])]

        def send(array, pairs):
            return lax.ppermute(array, AXES, pairs)

        def shared(array):
            return [array] + [send(array, across(t)) for t in range(1, cores)]

        def call(state, at, tail=None, part_of=(0, 1), last=False):
            keys, values = [every[0][b] for b in at], [every[1][b] for b in at]
            return attend(
                table,
                at,
                tail,
                part_of,
                info,
                queries,
                keys,
                values,
                shift,
                state,
                every if last else None,
                docs,
                span,
                kv_heads,
            )

        shift = shift_of(queries, keys, values, info, kv_heads)

        def arrived(begin, keys, values):
            every[0][begin : begin + len(keys)] = keys
            every[1][begin : begin + len(values)] = values
            return tuple(range(begin, begin + len(keys)))

        at = arrived(0, shared(keys), shared(values))
        state = call(None, at)
        kf = kb = keys
        vf = vb = values
        for s in steps:
            kf, kb = send(kf, forward), send(kb, backward)
            vf, vb = send(vf, forward), send(vb, backward)
            at = arrived(at[-1] + 1, shared(kf) + shared(kb), shared(vf) + shared(vb))
            if s < steps[-1]:
                for i in (0, 1):
                    state = call(state, at, None, (i, 2))
        s = steps[-1] + 1
        kf, vb = send(kf, forward), send(vb, backward)
        final = arrived(at[-1] + 1, shared(kf), shared(vb))
        mine_now = tuple(b for b in at if (b - at[0]) % cores == 0)
        swapped_now = tuple(b for b in at if b not in mine_now)
        tail = (mine_now, swapped_now, final)
        state = call(state, mine_now, tail)
        for i in (0, 1):
            state = call(state, at, tail, (i, 2))
        return call(state, swapped_now + final, tail, last=True)


    placed = P(("group", "seq", "head"), None)
    return jax.shard_map(
        local,
        mesh=mesh,
        in_specs=(placed, placed, placed, P("group"), P("group")),
        out_specs=placed,
        check_vma=False,
    )
```
